768 devices in a mesh: elem: 32 (over y, x), band: 24 (over z, core).
Axes of the slice: x: 4, y: 8, z: 12, core: 2. Of those that a mesh axis runs over, the one named last changes fastest.
Arguments:
- state: bfloat16 [393216, 256], P(('elem', 'band')), may hold values from -6 to 6
- dest_map: int32 [393216, 1], P(('elem', 'band')), may hold values from 0 to 31; in each aligned block of 512 rows (0 to 511, 512 to 1023, ...) at most 32 rows name the same one
- day_mask: int32 [393216, 1], P(('elem', 'band')), may hold values 0 or 1
- cloud: bfloat16 [786432, 512], P(('elem', 'band')), may hold values from -6 to 6
- conv_in: bfloat16 [768, 256], replicated, may hold values from -0.21875 to 0.21875
- conv_mid: bfloat16 [256, 256], replicated, may hold values from -0.375 to 0.375
- conv_out: bfloat16 [256, 768], replicated, may hold values from -0.375 to 0.375
- rad_in: bfloat16 [768, 256], replicated, may hold values from -0.21875 to 0.21875
- rad_mid: bfloat16 [256, 256], replicated, may hold values from -0.375 to 0.375
- rad_out: bfloat16 [256, 128], replicated, may hold values from -0.375 to 0.375
Outputs:
- tendency: bfloat16 [393216, 256], P(('elem', 'band'))
- new_cloud: bfloat16 [786432, 512], P(('elem', 'band'))
The draws below stay inside these ranges and needn't reach their ends.
Inputs may be any that keep to these rules, and one draw needn't show every extreme that they name: `dest_map`: among the columns of one device (aligned blocks of 512 rows) no value is named by more than 32 rows, a bound that some block reaches.
All inputs are finite; a program needn't handle non-finite values. No bound on the sum of `day_mask` on one device may be relied on, other than what follows from the above.
Results may differ from the reference program's by a relative error of at most 0.0058.
Values may be sent and summed in bfloat16 or wider, within the bound.
A program may use at most 32 MiB of HBM per device.

```python
import math
import jax
import jax.numpy as jnp
import numpy as np
from jax import lax

LEV = 128
HID = 256
COL_DEV = 512
CAP = 32
SLOTS = 1024
COLS = 393216
SPAN_ROWS = 786432
N_ELEM = 32
N_BAND = 24


def place_ends(values, rng, low, top_value):
    longest = values.shape.index(max(values.shape))
    spots = []
    for shift in (0, 1):
        where = [jax.random.randint(jax.random.fold_in(rng, axis), (), 0, length) for axis, length in enumerate(values.shape)]
        where[longest] = (where[longest] + shift) % values.shape[longest]
        spots.append(tuple(where))
    return values.at[spots[0]].set(low).at[spots[1]].set(top_value)


def block_levels(key, shape, shards, low, high):
    factor_of = 1.0
    for dim, blocks in shards:
        steps = jax.random.uniform(jax.random.fold_in(jax.random.fold_in(key, 6), dim), (blocks,), jnp.float32, low / len(shards), high / len(shards))
        factor_of = factor_of * jnp.repeat(jnp.exp(steps), shape[dim] // blocks).reshape((-1,) + (1,) * (len(shape) - 1 - dim))
    return factor_of


def shared_out(stream_key, own, number, rows, amount, top, most, skew):
    sequence = jax.random.permutation(stream_key, amount)
    packed, usual = shares(amount, rows * top, most, skew, True), shares(amount, rows * top, most, skew, False)
    places = jnp.arange(amount)

    def named(tallies, offset_by):
        used = int((tallies > 0).sum())
        fixed = max(1, used // 4)
        moved = fixed + (places - fixed + offset_by * (used - fixed)) % max(1, amount - fixed)
        return jnp.zeros((amount,), jnp.int32).at[sequence[jnp.where(places < fixed, places, moved)]].set(jnp.asarray(tallies, jnp.int32))

    tallies = jnp.where(number % 4 == 0, named(packed, number // 4), named(usual, number - number // 4 - 1))
    mixed = jax.random.permutation(jax.random.fold_in(own, 3), amount)
    giver, taker = mixed[0:amount // 2 * 2:2], mixed[1:amount // 2 * 2:2]
    margin = jnp.minimum(tallies[giver] - 1, most - tallies[taker]) // 2
    margin = jnp.where((giver == sequence[0]) | (taker == sequence[0]) | (tallies[taker] == 0), 0, jnp.maximum(margin, 0))
    moved = jax.random.randint(jax.random.fold_in(own, 4), (amount // 2,), 0, 1 << 20) % (margin + 1)
    tallies = tallies.at[giver].add(-moved).at[taker].add(moved)
    labels = jnp.searchsorted(jnp.cumsum(tallies), jnp.arange(rows * top), side="right").astype(jnp.int32)
    grid = labels.reshape(top, rows).T
    grid = grid[jax.random.permutation(jax.random.fold_in(own, 1), rows)]
    offset_by = jax.random.randint(jax.random.fold_in(own, 2), (rows, 1), 0, top)
    return jnp.take_along_axis(grid, (jnp.arange(top)[None, :] + offset_by) % top, axis=1)


def shares(amount, total, limit, slope, full):
    portions = [(1 << 20) // math.isqrt(rank ** slope) + 1 for rank in range(1, amount + 1)]
    largest = limit if full else min(limit, max(-(-total // amount), total * portions[0] // sum(portions)))
    least = 1 if total - largest >= amount - 1 else 0
    given, surplus = [largest] + [least] * (amount - 1), total - largest - least * (amount - 1)
    while surplus > 0:
        free = [i for i in range(1, amount) if given[i] < largest] or [i for i in range(1, amount) if given[i] < limit]
        pool, budget = sum([portions[i] for i in free]), surplus
        for i in free:
            more = min(limit - given[i], max(1, budget * portions[i] // pool), surplus)
            given[i] = given[i] + more
            surplus = surplus - more
    return np.array(given)


def noise(rng, dims, deviation, most, split=(), held_as=jnp.bfloat16):
    drawn = deviation * jax.random.normal(rng, dims, jnp.float32)
    if split:
        drawn = drawn * block_levels(rng, dims, split, -0.22, 0.18)
    return jnp.clip(drawn, -most, most).astype(held_as)


def setup_inputs(seed: int = 0) -> dict:
    arg_keys = jax.random.split(jax.random.key(seed), 11)
    state = noise(arg_keys[0], (COLS, 2 * LEV), 1.0, 6.0, ((0, 768),))
    dest_map_keys = jax.random.split(jax.random.fold_in(arg_keys[1], 1), COLS // COL_DEV)
    dest_map_turns = jax.random.permutation(jax.random.fold_in(arg_keys[1], 3), COLS // COL_DEV)
    dest_map = jax.vmap(lambda own, number: shared_out(jax.random.fold_in(arg_keys[1], 2), own, number, COL_DEV, N_ELEM, 1, CAP, 2))(dest_map_keys, dest_map_turns).reshape((COLS, 1))
    day_mask = place_ends((jax.random.randint(arg_keys[2], (COLS, 1), 0, 2) < 1).astype(jnp.int32), jax.random.fold_in(arg_keys[2], 1), 0, 1)
    cloud = noise(arg_keys[3], (SPAN_ROWS, 4 * LEV), 1.0, 6.0, ((0, 768),))
    conv_in = noise(arg_keys[4], (6 * LEV, HID), (6 * LEV) ** -0.5, 0.21875)
    conv_mid = noise(arg_keys[5], (HID, HID), HID ** -0.5, 0.375)
    conv_out = noise(arg_keys[6], (HID, 6 * LEV), HID ** -0.5, 0.375)
    rad_in = noise(arg_keys[7], (6 * LEV, HID), (6 * LEV) ** -0.5, 0.21875)
    rad_mid = noise(arg_keys[8], (HID, HID), HID ** -0.5, 0.375)
    rad_out = noise(arg_keys[9], (HID, LEV), HID ** -0.5, 0.375)
    return {"state": state, "dest_map": dest_map, "day_mask": day_mask, "cloud": cloud, "conv_in": conv_in, "conv_mid": conv_mid, "conv_out": conv_out, "rad_in": rad_in, "rad_mid": rad_mid, "rad_out": rad_out}


def column_physics(joined, daylight, cloud, conv_in, conv_mid, conv_out, rad_in, rad_mid, rad_out):
    conv_one = jax.nn.silu(jnp.dot(joined, conv_in, preferred_element_type=jnp.float32)).astype(jnp.bfloat16)
    conv_two = jax.nn.silu(jnp.dot(conv_one, conv_mid, preferred_element_type=jnp.float32)).astype(jnp.bfloat16)
    conv_result = jnp.dot(conv_two, conv_out, preferred_element_type=jnp.float32)
    rad_one = jax.nn.silu(jnp.dot(joined, rad_in, preferred_element_type=jnp.float32)).astype(jnp.bfloat16)
    rad_two = jax.nn.silu(jnp.dot(rad_one, rad_mid, preferred_element_type=jnp.float32)).astype(jnp.bfloat16)
    rad_result = jnp.dot(rad_two, rad_out, preferred_element_type=jnp.float32)
    heating = daylight[:, None] * rad_result
    padded = jnp.concatenate([heating, jnp.zeros_like(heating)], axis=1)
    tendency_rows = (conv_result[:, :2 * LEV] + padded).astype(jnp.bfloat16)
    updated = (cloud.astype(jnp.float32) + conv_result[:, 2 * LEV:]).astype(jnp.bfloat16)
    return tendency_rows, updated


def reference(state, dest_map, day_mask, cloud, conv_in, conv_mid, conv_out, rad_in, rad_mid, rad_out):
    target = dest_map[:, 0].reshape(N_ELEM, N_BAND, COL_DEV)
    onehot = (target[..., None] == jnp.arange(N_ELEM, dtype=jnp.int32)).astype(jnp.int32)
    order_in = jnp.sum((jnp.cumsum(onehot, axis=2) - onehot) * onehot, axis=-1)
    elem_index = jnp.arange(N_ELEM, dtype=jnp.int32)[:, None, None]
    band_index = jnp.arange(N_BAND, dtype=jnp.int32)[None, :, None]
    served_band = jnp.where(elem_index >= N_ELEM // 2, (band_index + N_BAND // 2) % N_BAND, band_index)
    span_row = ((target * N_BAND + served_band) * SLOTS + elem_index * CAP + order_in).reshape(-1).astype(jnp.int32)
    span_state = jnp.zeros((SPAN_ROWS, 2 * LEV), jnp.bfloat16).at[span_row].set(state)
    span_day = jnp.zeros((SPAN_ROWS,), jnp.float32).at[span_row].set(day_mask[:, 0].astype(jnp.float32))
    blocks = N_ELEM * N_BAND

    def one_block(pieces):
        block_state, block_day, block_cloud = pieces
        joined = jnp.concatenate([block_state, block_cloud], axis=1)
        return column_physics(joined, block_day, block_cloud, conv_in, conv_mid, conv_out, rad_in, rad_mid, rad_out)

    span_tendency, new_cloud = lax.map(one_block, (span_state.reshape(blocks, SLOTS, 2 * LEV), span_day.reshape(blocks, SLOTS), cloud.reshape(blocks, SLOTS, 4 * LEV)))
    span_tendency = span_tendency.reshape(SPAN_ROWS, 2 * LEV)
    new_cloud = new_cloud.reshape(SPAN_ROWS, 4 * LEV)
    tendency = span_tendency[span_row]
    return tendency, new_cloud
```

```python
import jax
import jax.numpy as jnp
from jax import lax
from jax.experimental import pallas as pl
from jax.experimental.pallas import tpu as pltpu
from jax.sharding import PartitionSpec as P

MESH = pl.DeviceIdType.MESH
BF = jnp.bfloat16
F32 = jnp.float32

GROUPS, CAP, COLS, FEAT, HID, LEV, CLOUD = 32, 32, 512, 256, 256, 128, 512
HALF = GROUPS // 2
SLOTS = GROUPS * CAP
BANDS = 24
LEG = 6
CHUNK = 4
ROWS = CHUNK * CAP


def dot(a, b):
    return jnp.dot(a, b, preferred_element_type=F32)


def silu(v):
    return (0.5 * v) * (1.0 + jnp.tanh(0.5 * v))


def kernel(
    dest_ref, day_ref, state_hbm, cloud_hbm, cin_hbm, cmid_hbm, cout_hbm, rin_hbm, rmid_hbm, rout_hbm,
    tend_ref, newcloud_hbm,
    state, cloud, cin, cmid, cout, rin, rmid, rout,
    outgoing, sunlit, arrived, arrived_sun, relay, upper, upper_sun,
    results, second, back_relay, back_here, returned, first_part, select, new_cloud,
    load_sem, out_sem,
    plane_recv, sun_recv, leg1_recv, leg2_recv, upsun_recv, back1_recv, back2_recv, final_recv,
    plane_send, sun_send, leg1_send, leg2_send, upsun_send, back1_send, back2_send, final_send,
):
    e = lax.axis_index("elem")
    b = lax.axis_index("band")
    up = lax.rem(b + LEG, BANDS)
    down = lax.rem(b + BANDS - LEG, BANDS)
    partner = lax.rem(b + BANDS // 2, BANDS)

    def toward(k):
        return lax.rem(b + LEG + (BANDS - 2 * LEG) * lax.rem(k, 2), BANDS)

    loads = [
        pltpu.make_async_copy(src, dst, load_sem.at[i])
        for i, (src, dst) in enumerate(
            (
                (state_hbm, state), (cloud_hbm, cloud), (cin_hbm, cin), (rin_hbm, rin),
                (cmid_hbm, cmid), (rmid_hbm, rmid), (cout_hbm, cout), (rout_hbm, rout),
            )
        )
    ]
    for load in loads:
        load.start()

    barrier = pltpu.get_barrier_semaphore()

    def greet(k, carry):
        pl.semaphore_signal(barrier, inc=1, device_id=(lax.rem(e + k, GROUPS), b), device_id_type=MESH)
        return carry

    lax.fori_loop(1, GROUPS, greet, 0)
    for band in (up, down, partner):
        pl.semaphore_signal(barrier, inc=1, device_id=(e, band), device_id_type=MESH)

    target = dest_ref[...]
    named = (lax.broadcasted_iota(jnp.int32, (GROUPS, COLS), 0) == target).astype(F32)
    earlier = (
        lax.broadcasted_iota(jnp.int32, (COLS, COLS), 0) < lax.broadcasted_iota(jnp.int32, (COLS, COLS), 1)
    ).astype(F32).astype(BF)
    counts = dot(named.astype(BF), earlier)
    order = jnp.sum(counts * named, axis=0, keepdims=True)
    position = target * CAP + order.astype(jnp.int32)
    sun_named = (named * day_ref[...].astype(F32)).astype(BF)
    ranked = (lax.broadcasted_iota(jnp.int32, (128, COLS), 0) == order.astype(jnp.int32)).astype(F32).astype(BF)
    sunlit[:, 0, :] = lax.dot_general(sun_named, ranked, (((1,), (1,)), ((), ())), preferred_element_type=F32)

    loads[0].wait()

    def pack(c, carry):
        slot = lax.broadcasted_iota(jnp.int32, (ROWS, COLS), 0) + c * ROWS
        chosen = (slot == position).astype(F32).astype(BF)
        outgoing[pl.ds(c * CHUNK, CHUNK)] = dot(chosen, state[...]).astype(BF).reshape(CHUNK, CAP, FEAT)
        return carry

    lax.fori_loop(0, GROUPS // CHUNK, pack, 0)

    pl.semaphore_wait(barrier, GROUPS - 1 + 3)

    def plane_copy(d):
        return pltpu.make_async_remote_copy(
            src_ref=outgoing.at[d], dst_ref=arrived.at[e], send_sem=plane_send, recv_sem=plane_recv.at[e],
            device_id=(d, b), device_id_type=MESH,
        )

    def sun_copy(d):
        return pltpu.make_async_remote_copy(
            src_ref=sunlit.at[d], dst_ref=arrived_sun.at[e], send_sem=sun_send, recv_sem=sun_recv.at[e // HALF],
            device_id=(d, b), device_id_type=MESH,
        )

    def send_blocks():
        def one(k, carry):
            d = lax.rem(e + k, GROUPS)
            plane_copy(d).start()
            sun_copy(d).start()
            return carry

        pltpu.make_async_copy(outgoing.at[e], arrived.at[e], plane_recv.at[e]).start()
        pltpu.make_async_copy(sunlit.at[e], arrived_sun.at[e], sun_recv.at[e // HALF]).start()
        lax.fori_loop(1, GROUPS, one, 0)

    @pl.when(e >= HALF)
    def _():
        send_blocks()

    for load in loads[1:]:
        load.wait()

    def cloud_part(c, carry):
        rows = pl.ds(pl.multiple_of(c * ROWS, ROWS), ROWS)
        block = cloud[rows, :]
        first_part[rows, :HID] = dot(block, cin[FEAT:, :])
        first_part[rows, HID:] = dot(block, rin[FEAT:, :])
        return carry

    lax.fori_loop(0, GROUPS // CHUNK, cloud_part, 0)

    @pl.when(e < HALF)
    def _():
        send_blocks()

    def arrival(buffer, sem):
        return pltpu.make_async_copy(buffer, buffer, sem)

    def z_copy(src, dst, k, send_sem, recv_sem):
        return pltpu.make_async_remote_copy(
            src_ref=src, dst_ref=dst.at[k], send_sem=send_sem, recv_sem=recv_sem.at[k],
            device_id=(e, toward(k)), device_id_type=MESH,
        )

    def leg1(k, carry):
        arrival(arrived.at[HALF + k], plane_recv.at[HALF + k]).wait()
        z_copy(arrived.at[HALF + k], relay, k, leg1_send, leg1_recv).start()
        return carry

    lax.fori_loop(0, HALF, leg1, 0)
    arrival(arrived_sun.at[pl.ds(HALF, HALF)], sun_recv.at[1]).wait()
    up_sun = pltpu.make_async_remote_copy(
        src_ref=arrived_sun.at[pl.ds(HALF, HALF)], dst_ref=upper_sun, send_sem=upsun_send, recv_sem=upsun_recv,
        device_id=(e, partner), device_id_type=MESH,
    )
    up_sun.start()

    def leg2(k, carry):
        arrival(relay.at[k], leg1_recv.at[k]).wait()
        z_copy(relay.at[k], upper, k, leg2_send, leg2_recv).start()
        return carry

    lax.fori_loop(0, HALF, leg2, 0)

    def physics(c, half, states, suns):
        rows = pl.ds(pl.multiple_of((half * (HALF // CHUNK) + c) * ROWS, ROWS), ROWS)
        x = states[pl.ds(c * CHUNK, CHUNK)].reshape(ROWS, FEAT)
        row = lax.broadcasted_iota(jnp.int32, (ROWS, HALF), 0) // CAP + c * CHUNK
        source = (row == lax.broadcasted_iota(jnp.int32, (ROWS, HALF), 1)).astype(F32).astype(BF)
        spread = dot(source, suns.astype(BF))
        place = lax.rem(lax.broadcasted_iota(jnp.int32, (ROWS, 128), 0), CAP)
        own = place == lax.broadcasted_iota(jnp.int32, (ROWS, 128), 1)
        daylight = jnp.sum(jnp.where(own, spread, 0.0), axis=1, keepdims=True)
        conv_one = silu(first_part[rows, :HID] + dot(x, cin[:FEAT, :])).astype(BF)
        rad_one = silu(first_part[rows, HID:] + dot(x, rin[:FEAT, :])).astype(BF)
        conv_two = silu(dot(conv_one, cmid[...])).astype(BF)
        rad_two = silu(dot(rad_one, rmid[...])).astype(BF)
        second[rows, :] = conv_two
        conv_result = dot(conv_two, cout[:, : 2 * LEV])
        heating = daylight * dot(rad_two, rout[...])
        blocks = pl.ds((half * (HALF // CHUNK) + c) * CHUNK, CHUNK)
        results[blocks, :, :LEV] = (conv_result[:, :LEV] + heating).astype(BF).reshape(CHUNK, CAP, LEV)
        results[blocks, :, LEV:] = conv_result[:, LEV:].astype(BF).reshape(CHUNK, CAP, LEV)

    def final_copy(src, owner):
        return pltpu.make_async_remote_copy(
            src_ref=src, dst_ref=returned.at[e], send_sem=final_send, recv_sem=final_recv.at[e],
            device_id=(owner, b), device_id_type=MESH,
        )

    def hand_back(src, owner):
        @pl.when(owner != e)
        def _():
            final_copy(src, owner).start()

        @pl.when(owner == e)
        def _():
            pltpu.make_async_copy(src, returned.at[e], final_recv.at[e]).start()

    def lower_arrival(k, carry):
        arrival(arrived.at[k], plane_recv.at[k]).wait()
        return carry

    lax.fori_loop(0, HALF, lower_arrival, 0)
    arrival(arrived_sun.at[pl.ds(0, HALF)], sun_recv.at[0]).wait()

    def lower_chunk(c, carry):
        physics(c, 0, arrived, arrived_sun[:HALF, 0, :])

        def one(j, inner):
            owner = c * CHUNK + j
            hand_back(results.at[owner], owner)
            return inner

        lax.fori_loop(0, CHUNK, one, 0)
        return carry

    lax.fori_loop(0, HALF // CHUNK, lower_chunk, 0)

    up_sun.wait_recv()

    def upper_chunk(c, carry):
        def come(j, inner):
            k = c * CHUNK + j
            arrival(upper.at[k], leg2_recv.at[k]).wait()
            return inner

        lax.fori_loop(0, CHUNK, come, 0)
        physics(c, 1, upper, upper_sun[:, 0, :])

        def one(j, inner):
            k = c * CHUNK + j
            z_copy(results.at[HALF + k], back_relay, k, back1_send, back1_recv).start()
            return inner

        lax.fori_loop(0, CHUNK, one, 0)
        return carry

    lax.fori_loop(0, HALF // CHUNK, upper_chunk, 0)

    def back2(k, carry):
        arrival(back_relay.at[k], back1_recv.at[k]).wait()
        z_copy(back_relay.at[k], back_here, k, back2_send, back2_recv).start()
        return carry

    lax.fori_loop(0, HALF, back2, 0)

    def cloud_update(c, carry):
        rows = pl.ds(pl.multiple_of(c * ROWS, ROWS), ROWS)
        change = dot(second[rows, :], cout[:, 2 * LEV :])
        new_cloud[rows, :] = (cloud[rows, :].astype(F32) + change).astype(BF)
        return carry

    lax.fori_loop(0, GROUPS // CHUNK, cloud_update, 0)
    store = pltpu.make_async_copy(new_cloud, newcloud_hbm, out_sem)
    store.start()

    def final(k, carry):
        arrival(back_here.at[k], back2_recv.at[k]).wait()
        hand_back(back_here.at[k], HALF + k)
        return carry

    lax.fori_loop(0, HALF, final, 0)

    def selection(c, carry):
        rows = pl.ds(pl.multiple_of(c * ROWS, ROWS), ROWS)
        column = lax.broadcasted_iota(jnp.int32, (ROWS, COLS), 0) + c * ROWS
        same = column == lax.broadcasted_iota(jnp.int32, (ROWS, COLS), 1)
        place = jnp.sum(jnp.where(same, position.astype(F32), 0.0), axis=1, keepdims=True).astype(jnp.int32)
        select[rows, :] = (
            lax.broadcasted_iota(jnp.int32, (ROWS, SLOTS), 1) == place
        ).astype(F32).astype(BF)
        return carry

    lax.fori_loop(0, COLS // ROWS, selection, 0)

    def final_arrival(k, carry):
        arrival(returned.at[k], final_recv.at[k]).wait()
        return carry

    lax.fori_loop(0, GROUPS, final_arrival, 0)
    everything = returned[...].reshape(SLOTS, FEAT)

    def gather(c, carry):
        rows = pl.ds(pl.multiple_of(c * ROWS, ROWS), ROWS)
        tend_ref[rows, :] = dot(select[rows, :], everything).astype(BF)
        return carry

    lax.fori_loop(0, COLS // ROWS, gather, 0)

    store.wait()
    arrival(outgoing.at[pl.ds(0, GROUPS - 1)], plane_send).wait()
    arrival(sunlit.at[pl.ds(0, GROUPS - 1)], sun_send).wait()
    arrival(relay, leg1_send).wait()
    arrival(relay, leg2_send).wait()
    up_sun.wait_send()
    arrival(relay, back1_send).wait()
    arrival(relay, back2_send).wait()
    arrival(returned.at[pl.ds(0, GROUPS - 1)], final_send).wait()


def per_device(state, dest_map, day_mask, cloud, conv_in, conv_mid, conv_out, rad_in, rad_mid, rad_out):
    vmem = pl.BlockSpec(memory_space=pltpu.VMEM)
    hbm = pl.BlockSpec(memory_space=pl.ANY)
    dma = pltpu.SemaphoreType.DMA
    half = pltpu.VMEM((HALF, CAP, FEAT), BF)
    whole = pltpu.VMEM((GROUPS, CAP, FEAT), BF)
    tendency, new_cloud = pl.pallas_call(
        kernel,
        name="physics_remap",
        out_shape=(
            jax.ShapeDtypeStruct((COLS, FEAT), BF),
            jax.ShapeDtypeStruct((SLOTS, CLOUD), BF),
        ),
        in_specs=[vmem, vmem] + [hbm] * 8,
        out_specs=(vmem, hbm),
        scratch_shapes=[
            pltpu.VMEM((COLS, FEAT), BF),
            pltpu.VMEM((SLOTS, CLOUD), BF),
            pltpu.VMEM((FEAT + CLOUD, HID), BF),
            pltpu.VMEM((HID, HID), BF),
            pltpu.VMEM((HID, 6 * LEV), BF),
            pltpu.VMEM((FEAT + CLOUD, HID), BF),
            pltpu.VMEM((HID, HID), BF),
            pltpu.VMEM((HID, LEV), BF),
            whole,
            pltpu.VMEM((GROUPS, 1, 128), F32),
            whole,
            pltpu.VMEM((GROUPS, 1, 128), F32),
            half,
            half,
            pltpu.VMEM((HALF, 1, 128), F32),
            whole,
            pltpu.VMEM((SLOTS, HID), BF),
            half,
            half,
            whole,
            pltpu.VMEM((SLOTS, 2 * HID), F32),
            pltpu.VMEM((COLS, SLOTS), BF),
            pltpu.VMEM((SLOTS, CLOUD), BF),
            dma((8,)),
            dma,
            dma((GROUPS,)), dma((2,)), dma((HALF,)), dma((HALF,)), dma, dma((HALF,)), dma((HALF,)), dma((GROUPS,)),
            dma, dma, dma, dma, dma, dma, dma, dma,
        ],
        compiler_params=pltpu.CompilerParams(collective_id=0, has_side_effects=True),
    )(
        dest_map.reshape(1, COLS), day_mask.reshape(1, COLS), state, cloud,
        conv_in, conv_mid, conv_out, rad_in, rad_mid, rad_out,
    )
    return tendency, new_cloud


def solution(mesh):
    rows = P(("elem", "band"), None)
    return jax.shard_map(
        per_device,
        mesh=mesh,
        in_specs=(rows, rows, rows, rows, P(), P(), P(), P(), P(), P()),
        out_specs=(rows, rows),
        check_vma=False,
    )
```

```python
import jax
import jax.numpy as jnp
from jax import lax
from jax.experimental import pallas as pl
from jax.experimental.pallas import tpu as pltpu
from jax.sharding import PartitionSpec as P

MESH = pl.DeviceIdType.MESH
BF = jnp.bfloat16
F32 = jnp.float32

GROUPS, CAP, COLS, FEAT, HID, LEV, CLOUD = 32, 32, 512, 256, 256, 128, 512
HALF = GROUPS // 2
SLOTS = GROUPS * CAP
BANDS = 24
LEG = 6
PIECES = 4
CHUNK = 4
WIDTH, HEIGHT = 4, 8
ROWS = CHUNK * CAP


def dot(a, b):
    return jnp.dot(a, b, preferred_element_type=F32)


def silu(v):
    return (0.5 * v) * (1.0 + jnp.tanh(0.5 * v))


def kernel(
    dest_ref, day_ref, state_hbm, cloud_hbm, cin_hbm, cmid_hbm, cout_hbm, rin_hbm, rmid_hbm, rout_hbm,
    returned, position_ref, newcloud_hbm,
    state, cloud, cin, cmid, cout, rin, rmid, rout,
    outgoing, sunlit, arrived, arrived_sun, relay, upper, upper_sun,
    results, second, back_relay, back_here, first_part, new_cloud,
    load_sem, out_sem,
    plane_recv, sun_recv, leg1_recv, leg2_recv, upsun_recv, back1_recv, back2_recv, final_recv,
    plane_send, sun_send, leg1_send, leg2_send, upsun_send, back1_send, back2_send, final_send,
):
    e = lax.axis_index("elem")
    b = lax.axis_index("band")
    up = lax.rem(b + LEG, BANDS)
    down = lax.rem(b + BANDS - LEG, BANDS)
    partner = lax.rem(b + BANDS // 2, BANDS)

    y = e // WIDTH
    x = lax.rem(e, WIDTH)
    rising = ((y >= 2) & (y <= 5)).astype(jnp.int32)

    def nth(i):
        c = i // CHUNK
        return (c * rising + (HALF // CHUNK - 1 - c) * (1 - rising)) * CHUNK + lax.rem(x + WIDTH - lax.rem(i, CHUNK), WIDTH)

    def toward(k):
        return lax.rem(b + LEG + (BANDS - 2 * LEG) * lax.rem(k, 2), BANDS)

    loads = [
        pltpu.make_async_copy(src, dst, load_sem.at[i])
        for i, (src, dst) in enumerate(
            (
                (state_hbm, state), (cloud_hbm, cloud), (cin_hbm, cin), (rin_hbm, rin),
                (cmid_hbm, cmid), (rmid_hbm, rmid), (cout_hbm, cout), (rout_hbm, rout),
            )
        )
    ]
    for load in loads:
        load.start()

    barrier = pltpu.get_barrier_semaphore()

    def greet(k, carry):
        pl.semaphore_signal(barrier, inc=1, device_id=(lax.rem(e + k, GROUPS), b), device_id_type=MESH)
        return carry

    lax.fori_loop(1, GROUPS, greet, 0)
    for band in (up, down, partner):
        pl.semaphore_signal(barrier, inc=1, device_id=(e, band), device_id_type=MESH)

    target = dest_ref[...]
    named = (lax.broadcasted_iota(jnp.int32, (GROUPS, COLS), 0) == target).astype(F32)
    earlier = (
        lax.broadcasted_iota(jnp.int32, (COLS, COLS), 0) < lax.broadcasted_iota(jnp.int32, (COLS, COLS), 1)
    ).astype(F32).astype(BF)
    counts = dot(named.astype(BF), earlier)
    order = jnp.sum(counts * named, axis=0, keepdims=True)
    position = target * CAP + order.astype(jnp.int32)
    position_ref[...] = position
    sun_named = (named * day_ref[...].astype(F32)).astype(BF)
    ranked = (lax.broadcasted_iota(jnp.int32, (128, COLS), 0) == order.astype(jnp.int32)).astype(F32).astype(BF)
    sunlit[:, 0, :] = lax.dot_general(sun_named, ranked, (((1,), (1,)), ((), ())), preferred_element_type=F32)

    loads[0].wait()

    def pack(c, carry):
        slot = lax.broadcasted_iota(jnp.int32, (ROWS, COLS), 0) + c * ROWS
        chosen = (slot == position).astype(F32).astype(BF)
        outgoing[pl.ds(c * CHUNK, CHUNK)] = dot(chosen, state[...]).astype(BF).reshape(CHUNK, CAP, FEAT)
        return carry

    lax.fori_loop(0, GROUPS // CHUNK, pack, 0)

    pl.semaphore_wait(barrier, GROUPS - 1 + 3)

    def plane_copy(d):
        return pltpu.make_async_remote_copy(
            src_ref=outgoing.at[d], dst_ref=arrived.at[e], send_sem=plane_send, recv_sem=plane_recv.at[e],
            device_id=(d, b), device_id_type=MESH,
        )

    def sun_copy(d):
        return pltpu.make_async_remote_copy(
            src_ref=sunlit.at[d], dst_ref=arrived_sun.at[e], send_sem=sun_send, recv_sem=sun_recv.at[e // HALF],
            device_id=(d, b), device_id_type=MESH,
        )

    def send_blocks():
        def one(k, carry):
            step = (k // WIDTH + 1) // 2
            turn = lax.rem(k // WIDTH, 2)
            row = lax.rem(y + step * turn + (HEIGHT - step) * (1 - turn), HEIGHT)
            d = row * WIDTH + lax.rem(x + lax.rem(k, WIDTH), WIDTH)
            plane_copy(d).start()
            sun_copy(d).start()
            return carry

        pltpu.make_async_copy(outgoing.at[e], arrived.at[e], plane_recv.at[e]).start()
        pltpu.make_async_copy(sunlit.at[e], arrived_sun.at[e], sun_recv.at[e // HALF]).start()
        lax.fori_loop(1, GROUPS, one, 0)

    send_blocks()

    for load in loads[1:]:
        load.wait()

    def cloud_part(c, carry):
        rows = pl.ds(pl.multiple_of(c * ROWS, ROWS), ROWS)
        block = cloud[rows, :]
        first_part[rows, :HID] = dot(block, cin[FEAT:, :])
        first_part[rows, HID:] = dot(block, rin[FEAT:, :])
        return carry

    lax.fori_loop(0, GROUPS // CHUNK, cloud_part, 0)

    def arrival(buffer, sem):
        return pltpu.make_async_copy(buffer, buffer, sem)

    def z_copy(src, dst, k, send_sem, recv_sem):
        return pltpu.make_async_remote_copy(
            src_ref=src, dst_ref=dst.at[k], send_sem=send_sem, recv_sem=recv_sem.at[k],
            device_id=(e, toward(k)), device_id_type=MESH,
        )

    def leg1(i, carry):
        k = nth(i)
        arrival(arrived.at[HALF + k], plane_recv.at[HALF + k]).wait()
        z_copy(arrived.at[HALF + k], relay, k, leg1_send, leg1_recv).start()
        return carry

    lax.fori_loop(0, CHUNK, leg1, 0)
    up_sun = pltpu.make_async_remote_copy(
        src_ref=arrived_sun.at[pl.ds(HALF, HALF)], dst_ref=upper_sun, send_sem=upsun_send, recv_sem=upsun_recv,
        device_id=(e, partner), device_id_type=MESH,
    )
    def leg2(i, carry):
        k = nth(i)
        arrival(relay.at[k], leg1_recv.at[k]).wait()
        z_copy(relay.at[k], upper, k, leg2_send, leg2_recv).start()
        return carry

    def both(i, carry):
        leg1(CHUNK + i, carry)
        leg2(i, carry)
        return carry

    lax.fori_loop(0, HALF - CHUNK, both, 0)
    arrival(arrived_sun.at[pl.ds(HALF, HALF)], sun_recv.at[1]).wait()
    up_sun.start()
    lax.fori_loop(HALF - CHUNK, HALF, leg2, 0)

    def physics(c, half, states, suns):
        rows = pl.ds(pl.multiple_of((half * (HALF // CHUNK) + c) * ROWS, ROWS), ROWS)
        x = states[pl.ds(c * CHUNK, CHUNK)].reshape(ROWS, FEAT)
        row = lax.broadcasted_iota(jnp.int32, (ROWS, HALF), 0) // CAP + c * CHUNK
        source = (row == lax.broadcasted_iota(jnp.int32, (ROWS, HALF), 1)).astype(F32).astype(BF)
        spread = dot(source, suns.astype(BF))
        place = lax.rem(lax.broadcasted_iota(jnp.int32, (ROWS, 128), 0), CAP)
        own = place == lax.broadcasted_iota(jnp.int32, (ROWS, 128), 1)
        daylight = jnp.sum(jnp.where(own, spread, 0.0), axis=1, keepdims=True)
        conv_one = silu(first_part[rows, :HID] + dot(x, cin[:FEAT, :])).astype(BF)
        rad_one = silu(first_part[rows, HID:] + dot(x, rin[:FEAT, :])).astype(BF)
        conv_two = silu(dot(conv_one, cmid[...])).astype(BF)
        rad_two = silu(dot(rad_one, rmid[...])).astype(BF)
        second[rows, :] = conv_two
        conv_result = dot(conv_two, cout[:, : 2 * LEV])
        heating = daylight * dot(rad_two, rout[...])
        blocks = pl.ds((half * (HALF // CHUNK) + c) * CHUNK, CHUNK)
        results[blocks, :, :LEV] = (conv_result[:, :LEV] + heating).astype(BF).reshape(CHUNK, CAP, LEV)
        results[blocks, :, LEV:] = conv_result[:, LEV:].astype(BF).reshape(CHUNK, CAP, LEV)

    def final_copy(src, owner):
        return pltpu.make_async_remote_copy(
            src_ref=src, dst_ref=returned.at[e], send_sem=final_send, recv_sem=final_recv.at[e],
            device_id=(owner, b), device_id_type=MESH,
        )

    def hand_back(src, owner):
        @pl.when(owner != e)
        def _():
            final_copy(src, owner).start()

        @pl.when(owner == e)
        def _():
            pltpu.make_async_copy(src, returned.at[e], final_recv.at[e]).start()

    def lower_arrival(k, carry):
        arrival(arrived.at[k], plane_recv.at[k]).wait()
        return carry

    lax.fori_loop(0, HALF, lower_arrival, 0)
    arrival(arrived_sun.at[pl.ds(0, HALF)], sun_recv.at[0]).wait()

    def lower_chunk(c, carry):
        physics(c, 0, arrived, arrived_sun[:HALF, 0, :])

        def one(j, inner):
            owner = c * CHUNK + j
            hand_back(results.at[owner], owner)
            return inner

        lax.fori_loop(0, CHUNK, one, 0)
        return carry

    lax.fori_loop(0, HALF // CHUNK, lower_chunk, 0)

    up_sun.wait_recv()

    def upper_chunk(i, carry):
        def come(j, inner):
            k = nth(i * CHUNK + j)
            arrival(upper.at[k], leg2_recv.at[k]).wait()
            return inner

        lax.fori_loop(0, CHUNK, come, 0)
        physics(nth(i * CHUNK) // CHUNK, 1, upper, upper_sun[:, 0, :])

        def one(j, inner):
            k = nth(i * CHUNK + j)
            z_copy(results.at[HALF + k], back_relay, k, back1_send, back1_recv).start()
            return inner

        lax.fori_loop(0, CHUNK, one, 0)
        return carry

    lax.fori_loop(0, HALF // CHUNK, upper_chunk, 0)

    def back2(i, carry):
        k = nth(i)
        arrival(back_relay.at[k], back1_recv.at[k]).wait()
        z_copy(back_relay.at[k], back_here, k, back2_send, back2_recv).start()
        return carry

    lax.fori_loop(0, HALF, back2, 0)

    def cloud_update(c, carry):
        rows = pl.ds(pl.multiple_of(c * ROWS, ROWS), ROWS)
        change = dot(second[rows, :], cout[:, 2 * LEV :])
        new_cloud[rows, :] = (cloud[rows, :].astype(F32) + change).astype(BF)
        return carry

    lax.fori_loop(0, GROUPS // CHUNK, cloud_update, 0)
    store = pltpu.make_async_copy(new_cloud, newcloud_hbm, out_sem)
    store.start()

    def final(i, carry):
        k = nth(i)
        arrival(back_here.at[k], back2_recv.at[k]).wait()
        hand_back(back_here.at[k], HALF + k)
        return carry

    lax.fori_loop(0, HALF, final, 0)

    def final_arrival(k, carry):
        arrival(returned.at[k], final_recv.at[k]).wait()
        return carry

    lax.fori_loop(0, GROUPS, final_arrival, 0)
    store.wait()
    arrival(outgoing.at[pl.ds(0, GROUPS - 1)], plane_send).wait()
    arrival(sunlit.at[pl.ds(0, GROUPS - 1)], sun_send).wait()
    arrival(relay, leg1_send).wait()
    arrival(relay, leg2_send).wait()
    up_sun.wait_send()
    arrival(relay, back1_send).wait()
    arrival(relay, back2_send).wait()
    arrival(outgoing.at[pl.ds(0, GROUPS - 1)], final_send).wait()


def finish(position_ref, returned_hbm, cloud_hbm, tend_ref, newcloud_hbm, returned, cloud, in_sem, out_sem, load_sem):
    load = pltpu.make_async_copy(returned_hbm, returned, load_sem)
    load.start()
    pieces = [pl.ds(i * (SLOTS // PIECES), SLOTS // PIECES) for i in range(PIECES)]
    come = [pltpu.make_async_copy(cloud_hbm.at[p], cloud.at[p], in_sem.at[i]) for i, p in enumerate(pieces)]
    go = [pltpu.make_async_copy(cloud.at[p], newcloud_hbm.at[p], out_sem.at[i]) for i, p in enumerate(pieces)]
    for copy in come:
        copy.start()

    def place(c):
        column = lax.broadcasted_iota(jnp.int32, (ROWS, COLS), 0) + c * ROWS
        same = column == lax.broadcasted_iota(jnp.int32, (ROWS, COLS), 1)
        own = jnp.where(same, position_ref[...].astype(F32), 0.0)
        return jnp.sum(own, axis=1, keepdims=True).astype(jnp.int32)

    slots = lax.broadcasted_iota(jnp.int32, (ROWS, SLOTS), 1)
    places = [place(c) for c in range(COLS // ROWS)]
    for first, second in zip(come, go):
        first.wait()
        second.start()
    load.wait()
    for c in range(COLS // ROWS):
        select = (slots == places[c]).astype(F32).astype(BF)
        tend_ref[pl.ds(c * ROWS, ROWS), :] = dot(select, returned[...].reshape(SLOTS, FEAT)).astype(BF)
    for copy in go:
        copy.wait()


def per_device(state, dest_map, day_mask, cloud, conv_in, conv_mid, conv_out, rad_in, rad_mid, rad_out):
    vmem = pl.BlockSpec(memory_space=pltpu.VMEM)
    hbm = pl.BlockSpec(memory_space=pl.ANY)
    dma = pltpu.SemaphoreType.DMA
    half = pltpu.VMEM((HALF, CAP, FEAT), BF)
    whole = pltpu.VMEM((GROUPS, CAP, FEAT), BF)
    returned, position, new_cloud = pl.pallas_call(
        kernel,
        name="physics_remap",
        out_shape=(
            jax.ShapeDtypeStruct((GROUPS, CAP, FEAT), BF),
            jax.ShapeDtypeStruct((1, COLS), jnp.int32),
            jax.ShapeDtypeStruct((SLOTS, CLOUD), BF),
        ),
        in_specs=[vmem, vmem] + [hbm] * 8,
        out_specs=(hbm, vmem, hbm),
        scratch_shapes=[
            pltpu.VMEM((COLS, FEAT), BF),
            pltpu.VMEM((SLOTS, CLOUD), BF),
            pltpu.VMEM((FEAT + CLOUD, HID), BF),
            pltpu.VMEM((HID, HID), BF),
            pltpu.VMEM((HID, 6 * LEV), BF),
            pltpu.VMEM((FEAT + CLOUD, HID), BF),
            pltpu.VMEM((HID, HID), BF),
            pltpu.VMEM((HID, LEV), BF),
            whole,
            pltpu.VMEM((GROUPS, 1, 128), F32),
            whole,
            pltpu.VMEM((GROUPS, 1, 128), F32),
            half,
            half,
            pltpu.VMEM((HALF, 1, 128), F32),
            whole,
            pltpu.VMEM((SLOTS, HID), BF),
            half,
            half,
            pltpu.VMEM((SLOTS, 2 * HID), F32),
            pltpu.VMEM((SLOTS, CLOUD), BF),
            dma((8,)),
            dma,
            dma((GROUPS,)), dma((2,)), dma((HALF,)), dma((HALF,)), dma, dma((HALF,)), dma((HALF,)), dma((GROUPS,)),
            dma, dma, dma, dma, dma, dma, dma, dma,
        ],
        compiler_params=pltpu.CompilerParams(collective_id=0, has_side_effects=True),
    )(
        dest_map.reshape(1, COLS), day_mask.reshape(1, COLS), state, cloud,
        conv_in, conv_mid, conv_out, rad_in, rad_mid, rad_out,
    )
    return pl.pallas_call(
        finish,
        name="finish",
        out_shape=(
            jax.ShapeDtypeStruct((COLS, FEAT), BF),
            jax.ShapeDtypeStruct((SLOTS, CLOUD), BF),
        ),
        in_specs=[vmem, hbm, hbm],
        out_specs=(vmem, hbm),
        scratch_shapes=[whole, pltpu.VMEM((SLOTS, CLOUD), BF), dma((PIECES,)), dma((PIECES,)), dma],
    )(position, returned, new_cloud)


def solution(mesh):
    rows = P(("elem", "band"), None)
    return jax.shard_map(
        per_device,
        mesh=mesh,
        in_specs=(rows, rows, rows, rows, P(), P(), P(), P(), P(), P()),
        out_specs=(rows, rows),
        check_vma=False,
    )
```

```python
import jax
import jax.numpy as jnp
from jax import lax
from jax.experimental import pallas as pl
from jax.experimental.pallas import tpu as pltpu
from jax.sharding import PartitionSpec as P

MESH = pl.DeviceIdType.MESH
BF = jnp.bfloat16
F32 = jnp.float32

GROUPS, CAP, COLS, FEAT, HID, LEV, CLOUD = 32, 32, 512, 256, 256, 128, 512
HALF = GROUPS // 2
SLOTS = GROUPS * CAP
BANDS = 24
LEG = 6
ARRIVAL = [
    sum(place * 4**n for n, place in enumerate(order))
    for order in (
        (3, 2, 1, 0), (3, 2, 0, 1), (0, 3, 1, 2), (0, 1, 2, 3), (0, 1, 2, 3), (1, 0, 2, 3), (2, 1, 3, 0), (3, 2, 1, 0),
    )
]
CHUNK = 4
WIDTH, HEIGHT = 4, 8
ROWS = CHUNK * CAP


def dot(a, b):
    return jnp.dot(a, b, preferred_element_type=F32)


def silu(v):
    return (0.5 * v) * (1.0 + jnp.tanh(0.5 * v))


def kernel(
    dest_ref, day_ref, state_hbm, cloud_hbm, cin_hbm, cmid_hbm, cout_hbm, rin_hbm, rmid_hbm, rout_hbm,
    returned, select, new_cloud,
    state, cloud, cin, cmid, cout, rin, rmid, rout,
    outgoing, sunlit, arrived, arrived_sun, relay, upper, upper_sun,
    results, second, back_relay, back_here, first_part,
    load_sem,
    plane_recv, sun_recv, leg1_recv, leg2_recv, upsun_recv, back1_recv, back2_recv, final_recv,
    plane_send, sun_send, leg1_send, leg2_send, upsun_send, back1_send, back2_send, final_send,
):
    e = lax.axis_index("elem")
    b = lax.axis_index("band")
    up = lax.rem(b + LEG, BANDS)
    down = lax.rem(b + BANDS - LEG, BANDS)
    partner = lax.rem(b + BANDS // 2, BANDS)

    y = e // WIDTH
    x = lax.rem(e, WIDTH)
    code = sum((y == row).astype(jnp.int32) * digits for row, digits in enumerate(ARRIVAL))

    def nth(i):
        n = i // CHUNK
        weight = 1 + 3 * (n >= 1).astype(jnp.int32) + 12 * (n >= 2).astype(jnp.int32) + 48 * (n >= 3).astype(jnp.int32)
        return lax.rem(code // weight, 4) * CHUNK + lax.rem(x + WIDTH - lax.rem(i, CHUNK), WIDTH)

    def toward(k):
        return lax.rem(b + LEG + (BANDS - 2 * LEG) * lax.rem(k, 2), BANDS)

    barrier = pltpu.get_barrier_semaphore()

    def greet(k, carry):
        pl.semaphore_signal(barrier, inc=1, device_id=(lax.rem(e + k, GROUPS), b), device_id_type=MESH)
        return carry

    for band in (partner, up, down):
        pl.semaphore_signal(barrier, inc=1, device_id=(e, band), device_id_type=MESH)
    lax.fori_loop(1, GROUPS, greet, 0)

    loads = [
        pltpu.make_async_copy(src, dst, load_sem.at[i])
        for i, (src, dst) in enumerate(
            (
                (state_hbm, state), (cloud_hbm, cloud), (cin_hbm, cin), (rin_hbm, rin),
                (cmid_hbm, cmid), (rmid_hbm, rmid), (cout_hbm, cout), (rout_hbm, rout),
            )
        )
    ]
    for load in loads:
        load.start()

    target = dest_ref[...]
    named = (lax.broadcasted_iota(jnp.int32, (GROUPS, COLS), 0) == target).astype(F32)
    earlier = (
        lax.broadcasted_iota(jnp.int32, (COLS, COLS), 0) < lax.broadcasted_iota(jnp.int32, (COLS, COLS), 1)
    ).astype(F32).astype(BF)
    counts = dot(named.astype(BF), earlier)
    order = jnp.sum(counts * named, axis=0, keepdims=True)
    position = target * CAP + order.astype(jnp.int32)
    sun_named = (named * day_ref[...].astype(F32)).astype(BF)
    ranked = (lax.broadcasted_iota(jnp.int32, (128, COLS), 0) == order.astype(jnp.int32)).astype(F32).astype(BF)
    sunlit[:, 0, :] = lax.dot_general(sun_named, ranked, (((1,), (1,)), ((), ())), preferred_element_type=F32)

    loads[0].wait()

    def pack(c, carry):
        slot = lax.broadcasted_iota(jnp.int32, (ROWS, COLS), 0) + c * ROWS
        chosen = (slot == position).astype(F32).astype(BF)
        outgoing[pl.ds(c * CHUNK, CHUNK)] = dot(chosen, state[...]).astype(BF).reshape(CHUNK, CAP, FEAT)
        return carry

    lax.fori_loop(0, GROUPS // CHUNK, pack, 0)

    pl.semaphore_wait(barrier, GROUPS - 1 + 3)

    def plane_copy(d):
        return pltpu.make_async_remote_copy(
            src_ref=outgoing.at[d], dst_ref=arrived.at[e], send_sem=plane_send, recv_sem=plane_recv.at[e],
            device_id=(d, b), device_id_type=MESH,
        )

    def sun_copy(d):
        return pltpu.make_async_remote_copy(
            src_ref=sunlit.at[d], dst_ref=arrived_sun.at[e], send_sem=sun_send, recv_sem=sun_recv.at[e // HALF],
            device_id=(d, b), device_id_type=MESH,
        )

    def send_blocks():
        def one(k, carry):
            step = (k // WIDTH + 1) // 2
            turn = lax.rem(k // WIDTH, 2)
            row = lax.rem(y + step * turn + (HEIGHT - step) * (1 - turn), HEIGHT)
            d = row * WIDTH + lax.rem(x + lax.rem(k, WIDTH), WIDTH)
            plane_copy(d).start()
            sun_copy(d).start()
            return carry

        pltpu.make_async_copy(outgoing.at[e], arrived.at[e], plane_recv.at[e]).start()
        pltpu.make_async_copy(sunlit.at[e], arrived_sun.at[e], sun_recv.at[e // HALF]).start()
        lax.fori_loop(1, GROUPS, one, 0)

    send_blocks()

    for load in loads[1:]:
        load.wait()

    def cloud_part(c, carry):
        rows = pl.ds(pl.multiple_of(c * ROWS, ROWS), ROWS)
        block = cloud[rows, :]
        first_part[rows, :HID] = dot(block, cin[FEAT:, :])
        first_part[rows, HID:] = dot(block, rin[FEAT:, :])
        return carry

    lax.fori_loop(0, GROUPS // CHUNK, cloud_part, 0)

    def arrival(buffer, sem):
        return pltpu.make_async_copy(buffer, buffer, sem)

    def z_copy(src, dst, k, send_sem, recv_sem):
        return pltpu.make_async_remote_copy(
            src_ref=src, dst_ref=dst.at[k], send_sem=send_sem, recv_sem=recv_sem.at[k],
            device_id=(e, toward(k)), device_id_type=MESH,
        )

    def leg1(i, carry):
        k = nth(i)
        arrival(arrived.at[HALF + k], plane_recv.at[HALF + k]).wait()
        z_copy(arrived.at[HALF + k], relay, k, leg1_send, leg1_recv).start()
        return carry

    lax.fori_loop(0, CHUNK, leg1, 0)
    up_sun = pltpu.make_async_remote_copy(
        src_ref=arrived_sun.at[pl.ds(HALF, HALF)], dst_ref=upper_sun, send_sem=upsun_send, recv_sem=upsun_recv,
        device_id=(e, partner), device_id_type=MESH,
    )
    def leg2(i, carry):
        k = nth(i)
        arrival(relay.at[k], leg1_recv.at[k]).wait()
        z_copy(relay.at[k], upper, k, leg2_send, leg2_recv).start()
        return carry

    def both(i, carry):
        leg1(CHUNK + i, carry)
        leg2(i, carry)
        return carry

    lax.fori_loop(0, HALF - CHUNK, both, 0)
    arrival(arrived_sun.at[pl.ds(HALF, HALF)], sun_recv.at[1]).wait()
    up_sun.start()
    lax.fori_loop(HALF - CHUNK, HALF, leg2, 0)

    def physics(c, half, states, suns):
        rows = pl.ds(pl.multiple_of((half * (HALF // CHUNK) + c) * ROWS, ROWS), ROWS)
        x = states[pl.ds(c * CHUNK, CHUNK)].reshape(ROWS, FEAT)
        row = lax.broadcasted_iota(jnp.int32, (ROWS, HALF), 0) // CAP + c * CHUNK
        source = (row == lax.broadcasted_iota(jnp.int32, (ROWS, HALF), 1)).astype(F32).astype(BF)
        spread = dot(source, suns.astype(BF))
        place = lax.rem(lax.broadcasted_iota(jnp.int32, (ROWS, 128), 0), CAP)
        own = place == lax.broadcasted_iota(jnp.int32, (ROWS, 128), 1)
        daylight = jnp.sum(jnp.where(own, spread, 0.0), axis=1, keepdims=True)
        conv_one = silu(first_part[rows, :HID] + dot(x, cin[:FEAT, :])).astype(BF)
        rad_one = silu(first_part[rows, HID:] + dot(x, rin[:FEAT, :])).astype(BF)
        conv_two = silu(dot(conv_one, cmid[...])).astype(BF)
        rad_two = silu(dot(rad_one, rmid[...])).astype(BF)
        second[rows, :] = conv_two
        conv_result = dot(conv_two, cout[:, : 2 * LEV])
        heating = daylight * dot(rad_two, rout[...])
        blocks = pl.ds((half * (HALF // CHUNK) + c) * CHUNK, CHUNK)
        results[blocks, :, :LEV] = (conv_result[:, :LEV] + heating).astype(BF).reshape(CHUNK, CAP, LEV)
        results[blocks, :, LEV:] = conv_result[:, LEV:].astype(BF).reshape(CHUNK, CAP, LEV)

    def final_copy(src, owner):
        return pltpu.make_async_remote_copy(
            src_ref=src, dst_ref=returned.at[e], send_sem=final_send, recv_sem=final_recv.at[e],
            device_id=(owner, b), device_id_type=MESH,
        )

    def hand_back(src, owner):
        @pl.when(owner != e)
        def _():
            final_copy(src, owner).start()

        @pl.when(owner == e)
        def _():
            pltpu.make_async_copy(src, returned.at[e], final_recv.at[e]).start()

    def lower_arrival(k, carry):
        arrival(arrived.at[k], plane_recv.at[k]).wait()
        return carry

    lax.fori_loop(0, HALF, lower_arrival, 0)
    arrival(arrived_sun.at[pl.ds(0, HALF)], sun_recv.at[0]).wait()

    def lower_chunk(c, carry):
        physics(c, 0, arrived, arrived_sun[:HALF, 0, :])

        def one(j, inner):
            owner = c * CHUNK + j
            hand_back(results.at[owner], owner)
            return inner

        lax.fori_loop(0, CHUNK, one, 0)
        return carry

    lax.fori_loop(0, HALF // CHUNK, lower_chunk, 0)

    up_sun.wait_recv()

    def upper_chunk(i, carry):
        def come(j, inner):
            k = nth(i * CHUNK + j)
            arrival(upper.at[k], leg2_recv.at[k]).wait()
            return inner

        lax.fori_loop(0, CHUNK, come, 0)
        physics(nth(i * CHUNK) // CHUNK, 1, upper, upper_sun[:, 0, :])

        def one(j, inner):
            k = nth(i * CHUNK + j)
            z_copy(results.at[HALF + k], back_relay, k, back1_send, back1_recv).start()
            return inner

        lax.fori_loop(0, CHUNK, one, 0)
        return carry

    lax.fori_loop(0, HALF // CHUNK, upper_chunk, 0)

    def back2(i, carry):
        k = nth(i)
        arrival(back_relay.at[k], back1_recv.at[k]).wait()
        z_copy(back_relay.at[k], back_here, k, back2_send, back2_recv).start()
        return carry

    lax.fori_loop(0, HALF, back2, 0)

    def cloud_update(c, carry):
        rows = pl.ds(pl.multiple_of(c * ROWS, ROWS), ROWS)
        change = dot(second[rows, :], cout[:, 2 * LEV :])
        new_cloud[rows, :] = (cloud[rows, :].astype(F32) + change).astype(BF)
        return carry

    lax.fori_loop(0, GROUPS // CHUNK, cloud_update, 0)

    def selection(c, carry):
        rows = pl.ds(pl.multiple_of(c * ROWS, ROWS), ROWS)
        column = lax.broadcasted_iota(jnp.int32, (ROWS, COLS), 0) + c * ROWS
        same = column == lax.broadcasted_iota(jnp.int32, (ROWS, COLS), 1)
        place = jnp.sum(jnp.where(same, position.astype(F32), 0.0), axis=1, keepdims=True).astype(jnp.int32)
        select[rows, :] = (lax.broadcasted_iota(jnp.int32, (ROWS, SLOTS), 1) == place).astype(F32).astype(BF)
        return carry

    lax.fori_loop(0, COLS // ROWS, selection, 0)

    def final(i, carry):
        k = nth(i)
        arrival(back_here.at[k], back2_recv.at[k]).wait()
        hand_back(back_here.at[k], HALF + k)
        return carry

    lax.fori_loop(0, HALF, final, 0)

    def final_arrival(k, carry):
        arrival(returned.at[k], final_recv.at[k]).wait()
        return carry

    lax.fori_loop(0, GROUPS, final_arrival, 0)
    arrival(outgoing.at[pl.ds(0, GROUPS - 1)], plane_send).wait()
    arrival(sunlit.at[pl.ds(0, GROUPS - 1)], sun_send).wait()
    arrival(relay, leg1_send).wait()
    arrival(relay, leg2_send).wait()
    up_sun.wait_send()
    arrival(relay, back1_send).wait()
    arrival(relay, back2_send).wait()
    arrival(outgoing.at[pl.ds(0, GROUPS - 1)], final_send).wait()


def finish(select, returned, cloud, tend_hbm, newcloud_hbm, tend, sem, tend_sem):
    store = pltpu.make_async_copy(cloud, newcloud_hbm, sem)
    store.start()
    outs = []
    for c in range(COLS // ROWS):
        rows = pl.ds(c * ROWS, ROWS)
        tend[rows, :] = dot(select[rows, :], returned[...].reshape(SLOTS, FEAT)).astype(BF)
        outs.append(pltpu.make_async_copy(tend.at[rows], tend_hbm.at[rows], tend_sem.at[c]))
        outs[-1].start()
    for out in outs:
        out.wait()
    store.wait()


def per_device(state, dest_map, day_mask, cloud, conv_in, conv_mid, conv_out, rad_in, rad_mid, rad_out):
    vmem = pl.BlockSpec(memory_space=pltpu.VMEM)
    hbm = pl.BlockSpec(memory_space=pl.ANY)
    dma = pltpu.SemaphoreType.DMA
    half = pltpu.VMEM((HALF, CAP, FEAT), BF)
    whole = pltpu.VMEM((GROUPS, CAP, FEAT), BF)
    returned, select, new_cloud = pl.pallas_call(
        kernel,
        name="physics_remap",
        out_shape=(
            whole,
            pltpu.VMEM((COLS, SLOTS), BF),
            pltpu.VMEM((SLOTS, CLOUD), BF),
        ),
        in_specs=[vmem, vmem] + [hbm] * 8,
        out_specs=(vmem, vmem, vmem),
        scratch_shapes=[
            pltpu.VMEM((COLS, FEAT), BF),
            pltpu.VMEM((SLOTS, CLOUD), BF),
            pltpu.VMEM((FEAT + CLOUD, HID), BF),
            pltpu.VMEM((HID, HID), BF),
            pltpu.VMEM((HID, 6 * LEV), BF),
            pltpu.VMEM((FEAT + CLOUD, HID), BF),
            pltpu.VMEM((HID, HID), BF),
            pltpu.VMEM((HID, LEV), BF),
            whole,
            pltpu.VMEM((GROUPS, 1, 128), F32),
            whole,
            pltpu.VMEM((GROUPS, 1, 128), F32),
            half,
            half,
            pltpu.VMEM((HALF, 1, 128), F32),
            whole,
            pltpu.VMEM((SLOTS, HID), BF),
            half,
            half,
            pltpu.VMEM((SLOTS, 2 * HID), F32),
            dma((8,)),
            dma((GROUPS,)), dma((2,)), dma((HALF,)), dma((HALF,)), dma, dma((HALF,)), dma((HALF,)), dma((GROUPS,)),
            dma, dma, dma, dma, dma, dma, dma, dma,
        ],
        compiler_params=pltpu.CompilerParams(collective_id=0, has_side_effects=True),
    )(
        dest_map.reshape(1, COLS), day_mask.reshape(1, COLS), state, cloud,
        conv_in, conv_mid, conv_out, rad_in, rad_mid, rad_out,
    )
    return pl.pallas_call(
        finish,
        name="finish",
        out_shape=(
            jax.ShapeDtypeStruct((COLS, FEAT), BF),
            jax.ShapeDtypeStruct((SLOTS, CLOUD), BF),
        ),
        in_specs=[vmem, vmem, vmem],
        out_specs=(hbm, hbm),
        scratch_shapes=[pltpu.VMEM((COLS, FEAT), BF), dma, dma((COLS // ROWS,))],
    )(pltpu.with_memory_space_constraint(select, pltpu.VMEM), pltpu.with_memory_space_constraint(returned, pltpu.VMEM), pltpu.with_memory_space_constraint(new_cloud, pltpu.VMEM))


def solution(mesh):
    rows = P(("elem", "band"), None)
    return jax.shard_map(
        per_device,
        mesh=mesh,
        in_specs=(rows, rows, rows, rows, P(), P(), P(), P(), P(), P()),
        out_specs=(rows, rows),
        check_vma=False,
    )
```

```python
import jax
import jax.numpy as jnp
from jax import lax
from jax.experimental import pallas as pl
from jax.experimental.pallas import tpu as pltpu
from jax.sharding import PartitionSpec as P

MESH = pl.DeviceIdType.MESH
BF = jnp.bfloat16
F32 = jnp.float32

GROUPS, CAP, COLS, FEAT, HID, LEV, CLOUD = 32, 32, 512, 256, 256, 128, 512
HALF = GROUPS // 2
SLOTS = GROUPS * CAP
BANDS = 24
LEG = 6
ARRIVAL = [
    sum(place * 4**n for n, place in enumerate(order))
    for order in (
        (3, 2, 1, 0), (3, 2, 0, 1), (0, 3, 1, 2), (0, 1, 2, 3), (0, 1, 2, 3), (1, 0, 2, 3), (2, 1, 3, 0), (3, 2, 1, 0),
    )
]
LAG = 1
CHUNK = 4
WIDTH, HEIGHT = 4, 8
ROWS = CHUNK * CAP


def dot(a, b):
    return jnp.dot(a, b, preferred_element_type=F32)


def silu(v):
    return (0.5 * v) * (1.0 + jnp.tanh(0.5 * v))


def kernel(
    dest_ref, day_ref, state_hbm, cloud_hbm, cin_hbm, cmid_hbm, cout_hbm, rin_hbm, rmid_hbm, rout_hbm,
    returned, select, new_cloud,
    state, cloud, cin, cmid, cout, rin, rmid, rout,
    outgoing, sunlit, arrived, arrived_sun, relay, upper, upper_sun,
    results, second, back_relay, back_here, first_part,
    load_sem,
    plane_recv, sun_recv, leg1_recv, leg2_recv, upsun_recv, back1_recv, back2_recv, final_recv,
    plane_send, sun_send, leg1_send, leg2_send, upsun_send, back1_send, back2_send, final_send,
):
    e = lax.axis_index("elem")
    b = lax.axis_index("band")
    up = lax.rem(b + LEG, BANDS)
    down = lax.rem(b + BANDS - LEG, BANDS)
    partner = lax.rem(b + BANDS // 2, BANDS)

    y = e // WIDTH
    x = lax.rem(e, WIDTH)
    code = sum((y == row).astype(jnp.int32) * digits for row, digits in enumerate(ARRIVAL))

    def nth(i):
        n = i // CHUNK
        weight = 1 + 3 * (n >= 1).astype(jnp.int32) + 12 * (n >= 2).astype(jnp.int32) + 48 * (n >= 3).astype(jnp.int32)
        return lax.rem(code // weight, 4) * CHUNK + lax.rem(x + WIDTH - lax.rem(i, CHUNK), WIDTH)

    def toward(k):
        return lax.rem(b + LEG + (BANDS - 2 * LEG) * lax.rem(k, 2), BANDS)

    barrier = pltpu.get_barrier_semaphore()

    def greet(k, carry):
        pl.semaphore_signal(barrier, inc=1, device_id=(lax.rem(e + k, GROUPS), b), device_id_type=MESH)
        return carry

    for band in (partner, up, down):
        pl.semaphore_signal(barrier, inc=1, device_id=(e, band), device_id_type=MESH)
    lax.fori_loop(1, GROUPS, greet, 0)

    loads = [
        pltpu.make_async_copy(src, dst, load_sem.at[i])
        for i, (src, dst) in enumerate(
            (
                (state_hbm, state), (cloud_hbm, cloud), (cin_hbm, cin), (rin_hbm, rin),
                (cmid_hbm, cmid), (rmid_hbm, rmid), (cout_hbm, cout), (rout_hbm, rout),
            )
        )
    ]
    for load in loads:
        load.start()

    target = dest_ref[...]
    named = (lax.broadcasted_iota(jnp.int32, (GROUPS, COLS), 0) == target).astype(F32)
    earlier = (
        lax.broadcasted_iota(jnp.int32, (COLS, COLS), 0) < lax.broadcasted_iota(jnp.int32, (COLS, COLS), 1)
    ).astype(F32).astype(BF)
    counts = dot(named.astype(BF), earlier)
    order = jnp.sum(counts * named, axis=0, keepdims=True)
    position = target * CAP + order.astype(jnp.int32)
    sun_named = (named * day_ref[...].astype(F32)).astype(BF)
    ranked = (lax.broadcasted_iota(jnp.int32, (128, COLS), 0) == order.astype(jnp.int32)).astype(F32).astype(BF)
    sunlit[:, 0, :] = lax.dot_general(sun_named, ranked, (((1,), (1,)), ((), ())), preferred_element_type=F32)

    loads[0].wait()

    def pack(c, carry):
        slot = lax.broadcasted_iota(jnp.int32, (ROWS, COLS), 0) + c * ROWS
        chosen = (slot == position).astype(F32).astype(BF)
        outgoing[pl.ds(c * CHUNK, CHUNK)] = dot(chosen, state[...]).astype(BF).reshape(CHUNK, CAP, FEAT)
        return carry

    lax.fori_loop(0, GROUPS // CHUNK, pack, 0)

    pl.semaphore_wait(barrier, GROUPS - 1 + 3)

    def plane_copy(d):
        return pltpu.make_async_remote_copy(
            src_ref=outgoing.at[d], dst_ref=arrived.at[e], send_sem=plane_send, recv_sem=plane_recv.at[e],
            device_id=(d, b), device_id_type=MESH,
        )

    def sun_copy(d):
        return pltpu.make_async_remote_copy(
            src_ref=sunlit.at[d], dst_ref=arrived_sun.at[e], send_sem=sun_send, recv_sem=sun_recv.at[e // CHUNK],
            device_id=(d, b), device_id_type=MESH,
        )

    def send_blocks():
        def one(k, carry):
            step = (k // WIDTH + 1) // 2
            turn = lax.rem(k // WIDTH, 2)
            row = lax.rem(y + step * turn + (HEIGHT - step) * (1 - turn), HEIGHT)
            d = row * WIDTH + lax.rem(x + lax.rem(k, WIDTH), WIDTH)
            plane_copy(d).start()
            sun_copy(d).start()
            return carry

        pltpu.make_async_copy(outgoing.at[e], arrived.at[e], plane_recv.at[e]).start()
        pltpu.make_async_copy(sunlit.at[e], arrived_sun.at[e], sun_recv.at[e // CHUNK]).start()
        lax.fori_loop(1, GROUPS, one, 0)

    send_blocks()

    for load in loads[1:]:
        load.wait()

    def cloud_part(c, carry):
        rows = pl.ds(pl.multiple_of(c * ROWS, ROWS), ROWS)
        block = cloud[rows, :]
        first_part[rows, :HID] = dot(block, cin[FEAT:, :])
        first_part[rows, HID:] = dot(block, rin[FEAT:, :])
        return carry

    lax.fori_loop(0, GROUPS // CHUNK, cloud_part, 0)

    def arrival(buffer, sem):
        return pltpu.make_async_copy(buffer, buffer, sem)

    def z_copy(src, dst, k, send_sem, recv_sem):
        return pltpu.make_async_remote_copy(
            src_ref=src, dst_ref=dst.at[k], send_sem=send_sem, recv_sem=recv_sem.at[k],
            device_id=(e, toward(k)), device_id_type=MESH,
        )

    def leg1(i, carry):
        k = nth(i)
        arrival(arrived.at[HALF + k], plane_recv.at[HALF + k]).wait()
        z_copy(arrived.at[HALF + k], relay, k, leg1_send, leg1_recv).start()
        return carry

    def sun_row(n):
        return nth(n * CHUNK) // CHUNK

    def up_sun(n):
        q = sun_row(n)
        rows = pl.ds(HALF + q * CHUNK, CHUNK)
        arrival(arrived_sun.at[rows], sun_recv.at[HALF // CHUNK + q]).wait()
        pltpu.make_async_remote_copy(
            src_ref=arrived_sun.at[rows], dst_ref=upper_sun.at[pl.ds(q * CHUNK, CHUNK)],
            send_sem=upsun_send, recv_sem=upsun_recv.at[q], device_id=(e, partner), device_id_type=MESH,
        ).start()

    def leg2(i, carry):
        k = nth(i)
        arrival(relay.at[k], leg1_recv.at[k]).wait()
        z_copy(relay.at[k], upper, k, leg2_send, leg2_recv).start()
        return carry

    def first_legs(n, carry):
        lax.fori_loop(n * CHUNK, (n + 1) * CHUNK, leg1, 0)
        up_sun(n)
        return carry

    def both_legs(n, carry):
        def both(i, inner):
            leg1(i, inner)
            leg2(i - LAG * CHUNK, inner)
            return inner

        lax.fori_loop(n * CHUNK, (n + 1) * CHUNK, both, 0)
        up_sun(n)
        return carry

    lax.fori_loop(0, LAG, first_legs, 0)
    lax.fori_loop(LAG, HALF // CHUNK, both_legs, 0)
    lax.fori_loop(HALF - LAG * CHUNK, HALF, leg2, 0)

    def physics(c, half, states, suns):
        rows = pl.ds(pl.multiple_of((half * (HALF // CHUNK) + c) * ROWS, ROWS), ROWS)
        x = states[pl.ds(c * CHUNK, CHUNK)].reshape(ROWS, FEAT)
        flags = suns[pl.ds(c * CHUNK, CHUNK), 0, :]
        spread = jnp.broadcast_to(flags[:, None, :], (CHUNK, CAP, 128)).reshape(ROWS, 128)
        place = lax.rem(lax.broadcasted_iota(jnp.int32, (ROWS, 128), 0), CAP)
        own = place == lax.broadcasted_iota(jnp.int32, (ROWS, 128), 1)
        daylight = jnp.sum(jnp.where(own, spread, 0.0), axis=1, keepdims=True)
        conv_one = silu(first_part[rows, :HID] + dot(x, cin[:FEAT, :])).astype(BF)
        rad_one = silu(first_part[rows, HID:] + dot(x, rin[:FEAT, :])).astype(BF)
        conv_two = silu(dot(conv_one, cmid[...])).astype(BF)
        rad_two = silu(dot(rad_one, rmid[...])).astype(BF)
        second[rows, :] = conv_two
        conv_result = dot(conv_two, cout[:, : 2 * LEV])
        heating = daylight * dot(rad_two, rout[...])
        blocks = pl.ds((half * (HALF // CHUNK) + c) * CHUNK, CHUNK)
        results[blocks, :, :LEV] = (conv_result[:, :LEV] + heating).astype(BF).reshape(CHUNK, CAP, LEV)
        results[blocks, :, LEV:] = conv_result[:, LEV:].astype(BF).reshape(CHUNK, CAP, LEV)

    def final_copy(src, owner):
        return pltpu.make_async_remote_copy(
            src_ref=src, dst_ref=returned.at[e], send_sem=final_send, recv_sem=final_recv.at[e],
            device_id=(owner, b), device_id_type=MESH,
        )

    def hand_back(src, owner):
        @pl.when(owner != e)
        def _():
            final_copy(src, owner).start()

        @pl.when(owner == e)
        def _():
            pltpu.make_async_copy(src, returned.at[e], final_recv.at[e]).start()

    def lower_arrival(k, carry):
        arrival(arrived.at[k], plane_recv.at[k]).wait()
        return carry

    lax.fori_loop(0, HALF, lower_arrival, 0)

    def lower_sun(q, carry):
        arrival(arrived_sun.at[pl.ds(q * CHUNK, CHUNK)], sun_recv.at[q]).wait()
        return carry

    lax.fori_loop(0, HALF // CHUNK, lower_sun, 0)

    def lower_chunk(c, carry):
        physics(c, 0, arrived, arrived_sun)

        def one(j, inner):
            owner = c * CHUNK + j
            hand_back(results.at[owner], owner)
            return inner

        lax.fori_loop(0, CHUNK, one, 0)
        return carry

    lax.fori_loop(0, HALF // CHUNK, lower_chunk, 0)

    def upper_chunk(i, carry):
        def come(j, inner):
            k = nth(i * CHUNK + j)
            arrival(upper.at[k], leg2_recv.at[k]).wait()
            return inner

        lax.fori_loop(0, CHUNK, come, 0)
        arrival(upper_sun.at[pl.ds(sun_row(i) * CHUNK, CHUNK)], upsun_recv.at[sun_row(i)]).wait()
        physics(nth(i * CHUNK) // CHUNK, 1, upper, upper_sun)

        def one(j, inner):
            k = nth(i * CHUNK + j)
            z_copy(results.at[HALF + k], back_relay, k, back1_send, back1_recv).start()
            return inner

        lax.fori_loop(0, CHUNK, one, 0)
        return carry

    lax.fori_loop(0, HALF // CHUNK, upper_chunk, 0)

    def back2(i, carry):
        k = nth(i)
        arrival(back_relay.at[k], back1_recv.at[k]).wait()
        z_copy(back_relay.at[k], back_here, k, back2_send, back2_recv).start()
        return carry

    lax.fori_loop(0, HALF, back2, 0)

    def cloud_update(c, carry):
        rows = pl.ds(pl.multiple_of(c * ROWS, ROWS), ROWS)
        change = dot(second[rows, :], cout[:, 2 * LEV :])
        new_cloud[rows, :] = (cloud[rows, :].astype(F32) + change).astype(BF)
        return carry

    lax.fori_loop(0, GROUPS // CHUNK, cloud_update, 0)

    def selection(c, carry):
        rows = pl.ds(pl.multiple_of(c * ROWS, ROWS), ROWS)
        column = lax.broadcasted_iota(jnp.int32, (ROWS, COLS), 0) + c * ROWS
        same = column == lax.broadcasted_iota(jnp.int32, (ROWS, COLS), 1)
        place = jnp.sum(jnp.where(same, position.astype(F32), 0.0), axis=1, keepdims=True).astype(jnp.int32)
        select[rows, :] = (lax.broadcasted_iota(jnp.int32, (ROWS, SLOTS), 1) == place).astype(F32).astype(BF)
        return carry

    lax.fori_loop(0, COLS // ROWS, selection, 0)

    def final(i, carry):
        k = nth(i)
        arrival(back_here.at[k], back2_recv.at[k]).wait()
        hand_back(back_here.at[k], HALF + k)
        return carry

    lax.fori_loop(0, HALF, final, 0)

    def final_arrival(k, carry):
        arrival(returned.at[k], final_recv.at[k]).wait()
        return carry

    lax.fori_loop(0, GROUPS, final_arrival, 0)
    arrival(outgoing.at[pl.ds(0, GROUPS - 1)], plane_send).wait()
    arrival(sunlit.at[pl.ds(0, GROUPS - 1)], sun_send).wait()
    arrival(relay, leg1_send).wait()
    arrival(relay, leg2_send).wait()
    arrival(upper_sun, upsun_send).wait()
    arrival(relay, back1_send).wait()
    arrival(relay, back2_send).wait()
    arrival(outgoing.at[pl.ds(0, GROUPS - 1)], final_send).wait()


def finish(select, returned, cloud, tend_hbm, newcloud_hbm, tend, sem, tend_sem):
    store = pltpu.make_async_copy(cloud, newcloud_hbm, sem)
    store.start()
    outs = []
    for c in range(COLS // ROWS):
        rows = pl.ds(c * ROWS, ROWS)
        tend[rows, :] = dot(select[rows, :], returned[...].reshape(SLOTS, FEAT)).astype(BF)
        outs.append(pltpu.make_async_copy(tend.at[rows], tend_hbm.at[rows], tend_sem.at[c]))
        outs[-1].start()
    for out in outs:
        out.wait()
    store.wait()


def per_device(state, dest_map, day_mask, cloud, conv_in, conv_mid, conv_out, rad_in, rad_mid, rad_out):
    vmem = pl.BlockSpec(memory_space=pltpu.VMEM)
    hbm = pl.BlockSpec(memory_space=pl.ANY)
    dma = pltpu.SemaphoreType.DMA
    half = pltpu.VMEM((HALF, CAP, FEAT), BF)
    whole = pltpu.VMEM((GROUPS, CAP, FEAT), BF)
    returned, select, new_cloud = pl.pallas_call(
        kernel,
        name="physics_remap",
        out_shape=(
            whole,
            pltpu.VMEM((COLS, SLOTS), BF),
            pltpu.VMEM((SLOTS, CLOUD), BF),
        ),
        in_specs=[vmem, vmem] + [hbm] * 8,
        out_specs=(vmem, vmem, vmem),
        scratch_shapes=[
            pltpu.VMEM((COLS, FEAT), BF),
            pltpu.VMEM((SLOTS, CLOUD), BF),
            pltpu.VMEM((FEAT + CLOUD, HID), BF),
            pltpu.VMEM((HID, HID), BF),
            pltpu.VMEM((HID, 6 * LEV), BF),
            pltpu.VMEM((FEAT + CLOUD, HID), BF),
            pltpu.VMEM((HID, HID), BF),
            pltpu.VMEM((HID, LEV), BF),
            whole,
            pltpu.VMEM((GROUPS, 1, 128), F32),
            whole,
            pltpu.VMEM((GROUPS, 1, 128), F32),
            half,
            half,
            pltpu.VMEM((HALF, 1, 128), F32),
            whole,
            pltpu.VMEM((SLOTS, HID), BF),
            half,
            half,
            pltpu.VMEM((SLOTS, 2 * HID), F32),
            dma((8,)),
            dma((GROUPS,)), dma((GROUPS // CHUNK,)), dma((HALF,)), dma((HALF,)), dma((HALF // CHUNK,)), dma((HALF,)), dma((HALF,)), dma((GROUPS,)),
            dma, dma, dma, dma, dma, dma, dma, dma,
        ],
        compiler_params=pltpu.CompilerParams(collective_id=0, has_side_effects=True),
    )(
        dest_map.reshape(1, COLS), day_mask.reshape(1, COLS), state, cloud,
        conv_in, conv_mid, conv_out, rad_in, rad_mid, rad_out,
    )
    return pl.pallas_call(
        finish,
        name="finish",
        out_shape=(
            jax.ShapeDtypeStruct((COLS, FEAT), BF),
            jax.ShapeDtypeStruct((SLOTS, CLOUD), BF),
        ),
        in_specs=[vmem, vmem, vmem],
        out_specs=(hbm, hbm),
        scratch_shapes=[pltpu.VMEM((COLS, FEAT), BF), dma, dma((COLS // ROWS,))],
    )(pltpu.with_memory_space_constraint(select, pltpu.VMEM), pltpu.with_memory_space_constraint(returned, pltpu.VMEM), pltpu.with_memory_space_constraint(new_cloud, pltpu.VMEM))


def solution(mesh):
    rows = P(("elem", "band"), None)
    return jax.shard_map(
        per_device,
        mesh=mesh,
        in_specs=(rows, rows, rows, rows, P(), P(), P(), P(), P(), P()),
        out_specs=(rows, rows),
        check_vma=False,
    )
```

```python
import jax
import jax.numpy as jnp
from jax import lax
from jax.experimental import pallas as pl
from jax.experimental.pallas import tpu as pltpu
from jax.sharding import PartitionSpec as P

MESH = pl.DeviceIdType.MESH
BF = jnp.bfloat16
F32 = jnp.float32

GROUPS, CAP, COLS, FEAT, HID, LEV, CLOUD = 32, 32, 512, 256, 256, 128, 512
HALF = GROUPS // 2
SLOTS = GROUPS * CAP
BANDS = 24
LEG = 6
ARRIVAL = [
    sum(place * 4**n for n, place in enumerate(order))
    for order in (
        (3, 2, 1, 0), (3, 2, 0, 1), (0, 3, 1, 2), (0, 1, 2, 3), (0, 1, 2, 3), (1, 0, 2, 3), (2, 1, 3, 0), (3, 2, 1, 0),
    )
]
LAG = 1
CHUNK = 4
WIDTH, HEIGHT = 4, 8
ROWS = CHUNK * CAP


def dot(a, b):
    return jnp.dot(a, b, preferred_element_type=F32)


def silu(v):
    return (0.5 * v) * (1.0 + jnp.tanh(0.5 * v))


def kernel(
    dest_ref, day_ref, state_hbm, cloud_hbm, cin_hbm, cmid_hbm, cout_hbm, rin_hbm, rmid_hbm, rout_hbm,
    returned, select, new_cloud,
    state, cloud, cin, cmid, cout, rin, rmid, rout,
    outgoing, sunlit, arrived, arrived_sun, relay, upper, upper_sun,
    results, second, back_relay, back_here, first_part,
    load_sem,
    plane_recv, sun_recv, leg1_recv, leg2_recv, upsun_recv, back1_recv, back2_recv, final_recv,
    plane_send, sun_send, leg1_send, leg2_send, upsun_send, back1_send, back2_send, final_send,
):
    e = lax.axis_index("elem")
    b = lax.axis_index("band")
    up = lax.rem(b + LEG, BANDS)
    down = lax.rem(b + BANDS - LEG, BANDS)
    partner = lax.rem(b + BANDS // 2, BANDS)

    y = e // WIDTH
    x = lax.rem(e, WIDTH)
    code = sum((y == row).astype(jnp.int32) * digits for row, digits in enumerate(ARRIVAL))

    def nth(i):
        n = i // CHUNK
        weight = 1 + 3 * (n >= 1).astype(jnp.int32) + 12 * (n >= 2).astype(jnp.int32) + 48 * (n >= 3).astype(jnp.int32)
        return lax.rem(code // weight, 4) * CHUNK + lax.rem(x + WIDTH - lax.rem(i, CHUNK), WIDTH)

    def toward(k):
        return lax.rem(b + LEG + (BANDS - 2 * LEG) * lax.rem(k, 2), BANDS)

    barrier = pltpu.get_barrier_semaphore()

    def greet(k, carry):
        pl.semaphore_signal(barrier, inc=1, device_id=(lax.rem(e + k, GROUPS), b), device_id_type=MESH)
        return carry

    for band in (partner, up, down):
        pl.semaphore_signal(barrier, inc=1, device_id=(e, band), device_id_type=MESH)
    lax.fori_loop(1, GROUPS, greet, 0)

    loads = [
        pltpu.make_async_copy(src, dst, load_sem.at[i])
        for i, (src, dst) in enumerate(
            (
                (state_hbm, state), (cloud_hbm, cloud), (cin_hbm, cin), (rin_hbm, rin),
                (cmid_hbm, cmid), (rmid_hbm, rmid), (cout_hbm, cout), (rout_hbm, rout),
            )
        )
    ]
    for load in loads:
        load.start()

    target = dest_ref[...]
    named = (lax.broadcasted_iota(jnp.int32, (GROUPS, COLS), 0) == target).astype(F32)
    earlier = (
        lax.broadcasted_iota(jnp.int32, (COLS, COLS), 0) < lax.broadcasted_iota(jnp.int32, (COLS, COLS), 1)
    ).astype(F32).astype(BF)
    counts = dot(named.astype(BF), earlier)
    order = jnp.sum(counts * named, axis=0, keepdims=True)
    position = target * CAP + order.astype(jnp.int32)
    sun_named = (named * day_ref[...].astype(F32)).astype(BF)
    ranked = (lax.broadcasted_iota(jnp.int32, (128, COLS), 0) == order.astype(jnp.int32)).astype(F32).astype(BF)
    sunlit[:, 0, :] = lax.dot_general(sun_named, ranked, (((1,), (1,)), ((), ())), preferred_element_type=F32)

    loads[0].wait()

    def pack(c, carry):
        slot = lax.broadcasted_iota(jnp.int32, (ROWS, COLS), 0) + c * ROWS
        chosen = (slot == position).astype(F32).astype(BF)
        outgoing[pl.ds(c * CHUNK, CHUNK)] = dot(chosen, state[...]).astype(BF).reshape(CHUNK, CAP, FEAT)
        return carry

    lax.fori_loop(0, GROUPS // CHUNK, pack, 0)

    pl.semaphore_wait(barrier, GROUPS - 1 + 3)

    def plane_copy(d):
        return pltpu.make_async_remote_copy(
            src_ref=outgoing.at[d], dst_ref=arrived.at[e], send_sem=plane_send, recv_sem=plane_recv.at[e],
            device_id=(d, b), device_id_type=MESH,
        )

    def sun_copy(d):
        return pltpu.make_async_remote_copy(
            src_ref=sunlit.at[d], dst_ref=arrived_sun.at[e], send_sem=sun_send, recv_sem=sun_recv.at[e // CHUNK],
            device_id=(d, b), device_id_type=MESH,
        )

    def send_blocks():
        def one(k, carry):
            step = (k // WIDTH + 1) // 2
            turn = lax.rem(k // WIDTH, 2)
            row = lax.rem(y + step * turn + (HEIGHT - step) * (1 - turn), HEIGHT)
            d = row * WIDTH + lax.rem(x + lax.rem(k, WIDTH), WIDTH)
            plane_copy(d).start()
            sun_copy(d).start()
            return carry

        pltpu.make_async_copy(outgoing.at[e], arrived.at[e], plane_recv.at[e]).start()
        pltpu.make_async_copy(sunlit.at[e], arrived_sun.at[e], sun_recv.at[e // CHUNK]).start()
        lax.fori_loop(1, GROUPS, one, 0)

    send_blocks()

    for load in loads[1:]:
        load.wait()

    def cloud_part(c, carry):
        rows = pl.ds(pl.multiple_of(c * ROWS, ROWS), ROWS)
        block = cloud[rows, :]
        first_part[rows, :HID] = dot(block, cin[FEAT:, :])
        first_part[rows, HID:] = dot(block, rin[FEAT:, :])
        return carry

    lax.fori_loop(0, GROUPS // CHUNK, cloud_part, 0)

    def arrival(buffer, sem):
        return pltpu.make_async_copy(buffer, buffer, sem)

    def z_copy(src, dst, k, send_sem, recv_sem):
        return pltpu.make_async_remote_copy(
            src_ref=src, dst_ref=dst.at[k], send_sem=send_sem, recv_sem=recv_sem.at[k],
            device_id=(e, toward(k)), device_id_type=MESH,
        )

    def leg1(i, carry):
        k = nth(i)
        arrival(arrived.at[HALF + k], plane_recv.at[HALF + k]).wait()
        z_copy(arrived.at[HALF + k], relay, k, leg1_send, leg1_recv).start()
        return carry

    def sun_row(n):
        return nth(n * CHUNK) // CHUNK

    def up_sun(n):
        q = sun_row(n)
        rows = pl.ds(HALF + q * CHUNK, CHUNK)
        arrival(arrived_sun.at[rows], sun_recv.at[HALF // CHUNK + q]).wait()
        pltpu.make_async_remote_copy(
            src_ref=arrived_sun.at[rows], dst_ref=upper_sun.at[pl.ds(q * CHUNK, CHUNK)],
            send_sem=upsun_send, recv_sem=upsun_recv.at[q], device_id=(e, partner), device_id_type=MESH,
        ).start()

    def leg2(i, carry):
        k = nth(i)
        arrival(relay.at[k], leg1_recv.at[k]).wait()
        z_copy(relay.at[k], upper, k, leg2_send, leg2_recv).start()
        return carry

    def first_legs(n, carry):
        lax.fori_loop(n * CHUNK, (n + 1) * CHUNK, leg1, 0)
        up_sun(n)
        return carry

    def both_legs(n, carry):
        def both(i, inner):
            leg1(i, inner)
            leg2(i - LAG * CHUNK, inner)
            return inner

        lax.fori_loop(n * CHUNK, (n + 1) * CHUNK, both, 0)
        up_sun(n)
        return carry

    lax.fori_loop(0, LAG, first_legs, 0)
    lax.fori_loop(LAG, HALF // CHUNK, both_legs, 0)
    lax.fori_loop(HALF - LAG * CHUNK, HALF, leg2, 0)

    def physics(c, half, states, suns):
        rows = pl.ds(pl.multiple_of((half * (HALF // CHUNK) + c) * ROWS, ROWS), ROWS)
        x = states[pl.ds(c * CHUNK, CHUNK)].reshape(ROWS, FEAT)
        flags = suns[pl.ds(c * CHUNK, CHUNK), 0, :]
        spread = jnp.broadcast_to(flags[:, None, :], (CHUNK, CAP, 128)).reshape(ROWS, 128)
        place = lax.rem(lax.broadcasted_iota(jnp.int32, (ROWS, 128), 0), CAP)
        own = place == lax.broadcasted_iota(jnp.int32, (ROWS, 128), 1)
        daylight = jnp.sum(jnp.where(own, spread, 0.0), axis=1, keepdims=True)
        conv_one = silu(first_part[rows, :HID] + dot(x, cin[:FEAT, :])).astype(BF)
        rad_one = silu(first_part[rows, HID:] + dot(x, rin[:FEAT, :])).astype(BF)
        conv_two = silu(dot(conv_one, cmid[...])).astype(BF)
        rad_two = silu(dot(rad_one, rmid[...])).astype(BF)
        second[rows, :] = conv_two
        conv_result = dot(conv_two, cout[:, : 2 * LEV])
        heating = daylight * dot(rad_two, rout[...])
        blocks = pl.ds((half * (HALF // CHUNK) + c) * CHUNK, CHUNK)
        results[blocks, :, :LEV] = (conv_result[:, :LEV] + heating).astype(BF).reshape(CHUNK, CAP, LEV)
        results[blocks, :, LEV:] = conv_result[:, LEV:].astype(BF).reshape(CHUNK, CAP, LEV)

    def final_copy(src, owner):
        return pltpu.make_async_remote_copy(
            src_ref=src, dst_ref=returned.at[e], send_sem=final_send, recv_sem=final_recv.at[e],
            device_id=(owner, b), device_id_type=MESH,
        )

    def hand_back(src, owner):
        @pl.when(owner != e)
        def _():
            final_copy(src, owner).start()

        @pl.when(owner == e)
        def _():
            pltpu.make_async_copy(src, returned.at[e], final_recv.at[e]).start()

    def lower_arrival(k, carry):
        arrival(arrived.at[k], plane_recv.at[k]).wait()
        return carry

    lax.fori_loop(0, HALF, lower_arrival, 0)

    def lower_sun(q, carry):
        arrival(arrived_sun.at[pl.ds(q * CHUNK, CHUNK)], sun_recv.at[q]).wait()
        return carry

    lax.fori_loop(0, HALF // CHUNK, lower_sun, 0)

    def lower_chunk(c, carry):
        physics(c, 0, arrived, arrived_sun)

        def one(j, inner):
            owner = c * CHUNK + j
            hand_back(results.at[owner], owner)
            return inner

        lax.fori_loop(0, CHUNK, one, 0)
        return carry

    lax.fori_loop(0, HALF // CHUNK, lower_chunk, 0)

    def upper_chunk(i, carry):
        def come(j, inner):
            k = nth(i * CHUNK + j)
            arrival(upper.at[k], leg2_recv.at[k]).wait()
            return inner

        lax.fori_loop(0, CHUNK, come, 0)
        arrival(upper_sun.at[pl.ds(sun_row(i) * CHUNK, CHUNK)], upsun_recv.at[sun_row(i)]).wait()
        physics(nth(i * CHUNK) // CHUNK, 1, upper, upper_sun)

        def one(j, inner):
            k = nth(i * CHUNK + j)
            z_copy(results.at[HALF + k], back_relay, k, back1_send, back1_recv).start()
            return inner

        lax.fori_loop(0, CHUNK, one, 0)
        return carry

    lax.fori_loop(0, HALF // CHUNK, upper_chunk, 0)

    def back2(i, carry):
        k = nth(i)
        arrival(back_relay.at[k], back1_recv.at[k]).wait()
        z_copy(back_relay.at[k], back_here, k, back2_send, back2_recv).start()
        return carry

    lax.fori_loop(0, HALF, back2, 0)

    def final(i, carry):
        k = nth(i)
        arrival(back_here.at[k], back2_recv.at[k]).wait()
        hand_back(back_here.at[k], HALF + k)
        return carry

    lax.fori_loop(0, HALF, final, 0)

    def cloud_update(c, carry):
        rows = pl.ds(pl.multiple_of(c * ROWS, ROWS), ROWS)
        change = dot(second[rows, :], cout[:, 2 * LEV :])
        new_cloud[rows, :] = (cloud[rows, :].astype(F32) + change).astype(BF)
        return carry

    lax.fori_loop(0, GROUPS // CHUNK, cloud_update, 0)

    def selection(c, carry):
        rows = pl.ds(pl.multiple_of(c * ROWS, ROWS), ROWS)
        column = lax.broadcasted_iota(jnp.int32, (ROWS, COLS), 0) + c * ROWS
        same = column == lax.broadcasted_iota(jnp.int32, (ROWS, COLS), 1)
        place = jnp.sum(jnp.where(same, position.astype(F32), 0.0), axis=1, keepdims=True).astype(jnp.int32)
        select[rows, :] = (lax.broadcasted_iota(jnp.int32, (ROWS, SLOTS), 1) == place).astype(F32).astype(BF)
        return carry

    lax.fori_loop(0, COLS // ROWS, selection, 0)

    def final_arrival(k, carry):
        arrival(returned.at[k], final_recv.at[k]).wait()
        return carry

    lax.fori_loop(0, GROUPS, final_arrival, 0)
    arrival(outgoing.at[pl.ds(0, GROUPS - 1)], plane_send).wait()
    arrival(sunlit.at[pl.ds(0, GROUPS - 1)], sun_send).wait()
    arrival(relay, leg1_send).wait()
    arrival(relay, leg2_send).wait()
    arrival(upper_sun, upsun_send).wait()
    arrival(relay, back1_send).wait()
    arrival(relay, back2_send).wait()
    arrival(outgoing.at[pl.ds(0, GROUPS - 1)], final_send).wait()


def finish(select, returned, cloud, tend_hbm, newcloud_hbm, tend, sem, tend_sem):
    store = pltpu.make_async_copy(cloud, newcloud_hbm, sem)
    store.start()
    outs = []
    for c in range(COLS // ROWS):
        rows = pl.ds(c * ROWS, ROWS)
        tend[rows, :] = dot(select[rows, :], returned[...].reshape(SLOTS, FEAT)).astype(BF)
        outs.append(pltpu.make_async_copy(tend.at[rows], tend_hbm.at[rows], tend_sem.at[c]))
        outs[-1].start()
    for out in outs:
        out.wait()
    store.wait()


def per_device(state, dest_map, day_mask, cloud, conv_in, conv_mid, conv_out, rad_in, rad_mid, rad_out):
    vmem = pl.BlockSpec(memory_space=pltpu.VMEM)
    hbm = pl.BlockSpec(memory_space=pl.ANY)
    dma = pltpu.SemaphoreType.DMA
    half = pltpu.VMEM((HALF, CAP, FEAT), BF)
    whole = pltpu.VMEM((GROUPS, CAP, FEAT), BF)
    returned, select, new_cloud = pl.pallas_call(
        kernel,
        name="physics_remap",
        out_shape=(
            whole,
            pltpu.VMEM((COLS, SLOTS), BF),
            pltpu.VMEM((SLOTS, CLOUD), BF),
        ),
        in_specs=[vmem, vmem] + [hbm] * 8,
        out_specs=(vmem, vmem, vmem),
        scratch_shapes=[
            pltpu.VMEM((COLS, FEAT), BF),
            pltpu.VMEM((SLOTS, CLOUD), BF),
            pltpu.VMEM((FEAT + CLOUD, HID), BF),
            pltpu.VMEM((HID, HID), BF),
            pltpu.VMEM((HID, 6 * LEV), BF),
            pltpu.VMEM((FEAT + CLOUD, HID), BF),
            pltpu.VMEM((HID, HID), BF),
            pltpu.VMEM((HID, LEV), BF),
            whole,
            pltpu.VMEM((GROUPS, 1, 128), F32),
            whole,
            pltpu.VMEM((GROUPS, 1, 128), F32),
            half,
            half,
            pltpu.VMEM((HALF, 1, 128), F32),
            whole,
            pltpu.VMEM((SLOTS, HID), BF),
            half,
            half,
            pltpu.VMEM((SLOTS, 2 * HID), F32),
            dma((8,)),
            dma((GROUPS,)), dma((GROUPS // CHUNK,)), dma((HALF,)), dma((HALF,)), dma((HALF // CHUNK,)), dma((HALF,)), dma((HALF,)), dma((GROUPS,)),
            dma, dma, dma, dma, dma, dma, dma, dma,
        ],
        compiler_params=pltpu.CompilerParams(collective_id=0, has_side_effects=True),
    )(
        dest_map.reshape(1, COLS), day_mask.reshape(1, COLS), state, cloud,
        conv_in, conv_mid, conv_out, rad_in, rad_mid, rad_out,
    )
    return pl.pallas_call(
        finish,
        name="finish",
        out_shape=(
            jax.ShapeDtypeStruct((COLS, FEAT), BF),
            jax.ShapeDtypeStruct((SLOTS, CLOUD), BF),
        ),
        in_specs=[vmem, vmem, vmem],
        out_specs=(hbm, hbm),
        scratch_shapes=[pltpu.VMEM((COLS, FEAT), BF), dma, dma((COLS // ROWS,))],
    )(pltpu.with_memory_space_constraint(select, pltpu.VMEM), pltpu.with_memory_space_constraint(returned, pltpu.VMEM), pltpu.with_memory_space_constraint(new_cloud, pltpu.VMEM))


def solution(mesh):
    rows = P(("elem", "band"), None)
    return jax.shard_map(
        per_device,
        mesh=mesh,
        in_specs=(rows, rows, rows, rows, P(), P(), P(), P(), P(), P()),
        out_specs=(rows, rows),
        check_vma=False,
    )
```
